32 devices in a mesh: tm: 4 (over y, x), seq: 8 (over z, core).
Axes of the slice: x: 2, y: 2, z: 4, core: 2. Of those that a mesh axis runs over, the one named last changes fastest.
Arguments:
- queries: bfloat16 [4, 1024, 1024], P('tm', 'seq'), may hold values from -5 to 5
- keys: bfloat16 [4, 1024, 1024], P('tm', 'seq'), may hold values from -5 to 5
- values: bfloat16 [4, 1024, 1024], P('tm', 'seq'), may hold values from -6 to 6
- grad_out: bfloat16 [4, 1024, 1024], P('tm', 'seq'), may hold values from -6 to 6
- block_mask: int32 [4, 8, 6], P('tm', 'seq'), may hold values from 0 to 1, as said below
- valid_len: int32 [4], replicated, may hold values from 512 to 1024, as said below
Outputs:
- grad_query: bfloat16 [4, 1024, 1024], P('tm', 'seq')
- grad_key: bfloat16 [4, 1024, 1024], P('tm', 'seq')
- grad_value: bfloat16 [4, 1024, 1024], P('tm', 'seq')
The draws below stay inside these ranges and needn't reach their ends.
Inputs may be any that keep to these rules, and one draw needn't show every extreme that they name: `block_mask`: entry 1 (a query block's own block) is always 1. `valid_len`: some frame is complete.
All inputs are finite; a program needn't handle non-finite values.
Results may differ from the reference program's by a relative error of at most 0.022.
Values may be sent and summed in bfloat16 or wider, within the bound.
A program may use at most 64 MiB of HBM per device.

```python
import jax
import jax.numpy as jnp
from jax import lax

HEADS = 8
HD = 128
BLK = 128
FRAMES = 4
NBLK = 8
FRAME_TOK = 1024
FEAT = 1024


def draw_queries(key, part):
    array_dims = (FRAMES, NBLK, BLK, HEADS * HD)
    sample = jnp.clip(jax.random.normal(jax.random.fold_in(key, 1), array_dims, jnp.float32), -4.5, 4.5)
    return sample.reshape(FRAMES, FRAME_TOK, HEADS * HD).astype(jnp.bfloat16)


def draw_keys(key, part):
    array_dims = (FRAMES, NBLK, BLK, HEADS * HD)
    sample = jnp.clip(jax.random.normal(jax.random.fold_in(key, 2), array_dims, jnp.float32), -4.5, 4.5)
    return sample.reshape(FRAMES, FRAME_TOK, HEADS * HD).astype(jnp.bfloat16)


def draw_block_mask(key, part):
    coin_flips = jax.random.randint(jax.random.fold_in(key, 5), (FRAMES, NBLK, 6), 0, 2)
    own_entry = (jnp.arange(6) == 1)[None, None, :]
    return jnp.where(own_entry, 1, coin_flips).astype(jnp.int32)


def draw_valid_len(key, part):
    counts = jax.random.randint(jax.random.fold_in(key, 3), (FRAMES,), FRAME_TOK // 2, FRAME_TOK + 1)
    complete = jax.random.randint(jax.random.fold_in(key, 4), (), 0, FRAMES)
    return jnp.where(jnp.arange(FRAMES) == complete, FRAME_TOK, counts).astype(jnp.int32)


def block_levels(own_key, extent, shards, smallest, largest):
    gain = 1.0
    for position, parts in shards:
        draws = jax.random.uniform(jax.random.fold_in(jax.random.fold_in(own_key, 6), position), (parts,), jnp.float32, smallest / len(shards), largest / len(shards))
        gain = gain * jnp.repeat(jnp.exp(draws), extent[position] // parts).reshape((-1,) + (1,) * (len(extent) - 1 - position))
    return gain


def gaussian(key, dims, deviation, bound, shards=(), kind=jnp.bfloat16):
    values = jax.random.normal(key, dims, jnp.float32) * deviation
    if len(shards) > 0:
        values = block_levels(key, dims, shards, -0.22, 0.18) * values
    return jnp.clip(values, min=-bound, max=bound).astype(kind)


def setup_inputs(seed: int = 0) -> dict:
    key_list = jax.random.split(jax.random.key(seed), 7)
    queries = draw_queries(jax.random.fold_in(key_list[6], 71), 0)
    keys = draw_keys(jax.random.fold_in(key_list[6], 71), 0)
    values = gaussian(key_list[2], (FRAMES, FRAME_TOK, FEAT), 1.0, 6.0, ((0, 4), (1, 8)))
    grad_out = gaussian(key_list[3], (FRAMES, FRAME_TOK, FEAT), 1.0, 6.0, ((0, 4), (1, 8)))
    block_mask = draw_block_mask(jax.random.fold_in(key_list[6], 71), 0)
    valid_len = draw_valid_len(jax.random.fold_in(key_list[6], 71), 0)
    return dict(queries=queries, keys=keys, values=values, grad_out=grad_out, block_mask=block_mask, valid_len=valid_len)


def attend_block(query_blk, key_ext, value_ext, grad_blk, allowed, query_ok):
    feat_dim = query_blk.shape[-1]
    head_dim = feat_dim // HEADS
    scaling = head_dim ** -0.5
    query_heads = query_blk.astype(jnp.float32).reshape(BLK, HEADS, head_dim)
    key_heads = key_ext.astype(jnp.float32).reshape(6 * BLK, HEADS, head_dim)
    value_heads = value_ext.astype(jnp.float32).reshape(6 * BLK, HEADS, head_dim)
    scores = scaling * jnp.einsum('ihd,jhd->hij', query_heads, key_heads)
    masked = jnp.where(allowed[None, None, :], scores, -1e30)
    row_max = jnp.max(masked, axis=-1, keepdims=True)
    log_total = row_max + jnp.log(jnp.sum(jnp.exp(masked - row_max), axis=-1, keepdims=True))
    prob_f32 = jnp.exp(masked - log_total)
    prob_bf = lax.optimization_barrier(prob_f32.astype(jnp.bfloat16)).astype(jnp.float32)
    attended = jnp.einsum('hij,jhd->ihd', prob_bf, value_heads)
    okay = query_ok.astype(jnp.float32)[:, None, None]
    attended_bf = lax.optimization_barrier((attended * okay).astype(jnp.bfloat16)).astype(jnp.float32)
    grad_in = grad_blk.astype(jnp.float32).reshape(BLK, HEADS, head_dim) * okay
    row_dot = jnp.sum(grad_in * attended_bf, axis=-1)
    dprob = jnp.einsum('ihd,jhd->hij', grad_in, value_heads)
    dscore = prob_f32 * (dprob - jnp.transpose(row_dot)[:, :, None])
    dscore = lax.optimization_barrier(dscore.astype(jnp.bfloat16)).astype(jnp.float32)
    grad_query = (scaling * jnp.einsum('hij,jhd->ihd', dscore, key_heads)).astype(jnp.bfloat16)
    grad_key = scaling * jnp.einsum('hij,ihd->jhd', dscore, query_heads)
    grad_value = jnp.einsum('hij,ihd->jhd', prob_bf, grad_in)
    return (grad_query.reshape(BLK, feat_dim), grad_key.reshape(6 * BLK, feat_dim),
            grad_value.reshape(6 * BLK, feat_dim))


def reference(queries, keys, values, grad_out, block_mask, valid_len):
    frames = queries.shape[0]
    feat_dim = queries.shape[2]
    blocks_all = queries.shape[1] // BLK

    def split(array):
        return array.reshape(frames, blocks_all, BLK, feat_dim)

    key_pad = jnp.pad(split(keys), ((1, 0), (1, 1), (0, 0), (0, 0)))
    value_pad = jnp.pad(split(values), ((1, 0), (1, 1), (0, 0), (0, 0)))
    query_blocks = split(queries)
    grad_blocks = split(grad_out)
    candidate = jnp.arange(6, dtype=jnp.int32)
    inside = jnp.arange(BLK, dtype=jnp.int32)
    zero = jnp.zeros((), jnp.int32)

    def add_at(accum, piece, frame_pos, block_pos):
        start = (frame_pos, block_pos, zero, zero)
        current = lax.dynamic_slice(accum, start, (1, 3, BLK, feat_dim))
        return lax.dynamic_update_slice(accum, current + piece[None], start)

    def neighbours(padded, frame_idx, block_idx):
        own_part = lax.dynamic_slice(padded, (frame_idx + 1, block_idx, zero, zero), (1, 3, BLK, feat_dim))[0]
        prev_part = lax.dynamic_slice(padded, (frame_idx, block_idx, zero, zero), (1, 3, BLK, feat_dim))[0]
        return jnp.concatenate((own_part, prev_part), axis=0).reshape(6 * BLK, feat_dim)

    def step(carry, step_index):
        key_acc, value_acc = carry
        frame_idx = step_index // blocks_all
        block_idx = step_index % blocks_all
        query_blk = query_blocks[frame_idx, block_idx]
        grad_blk = grad_blocks[frame_idx, block_idx]
        key_ext = neighbours(key_pad, frame_idx, block_idx)
        value_ext = neighbours(value_pad, frame_idx, block_idx)
        near_block = block_idx + candidate % 3 - 1
        src_frame = frame_idx - candidate // 3
        src_valid = valid_len[jnp.clip(src_frame, 0, frames - 1)]
        positions = near_block[:, None] * BLK + inside[None, :]
        block_ok = (block_mask[frame_idx, block_idx] == 1) & (near_block >= 0) & (near_block < blocks_all) & (src_frame >= 0)
        allowed = (block_ok[:, None] & (positions < src_valid[:, None])).reshape(6 * BLK)
        query_ok = block_idx * BLK + inside < valid_len[frame_idx]
        grad_query, grad_key, grad_value = attend_block(query_blk, key_ext, value_ext, grad_blk, allowed, query_ok)
        grad_key = grad_key.reshape(2, 3, BLK, feat_dim)
        grad_value = grad_value.reshape(2, 3, BLK, feat_dim)
        key_acc = add_at(add_at(key_acc, grad_key[0], frame_idx + 1, block_idx), grad_key[1], frame_idx, block_idx)
        value_acc = add_at(add_at(value_acc, grad_value[0], frame_idx + 1, block_idx), grad_value[1], frame_idx, block_idx)
        return (key_acc, value_acc), grad_query

    start_acc = jnp.zeros(key_pad.shape, jnp.float32)
    (key_acc, value_acc), query_parts = lax.scan(step, (start_acc, start_acc), jnp.arange(frames * blocks_all, dtype=jnp.int32))
    grad_query = query_parts.reshape(frames, blocks_all * BLK, feat_dim)
    grad_key = key_acc[1:, 1:-1].reshape(frames, blocks_all * BLK, feat_dim).astype(jnp.bfloat16)
    grad_value = value_acc[1:, 1:-1].reshape(frames, blocks_all * BLK, feat_dim).astype(jnp.bfloat16)
    return (grad_query, grad_key, grad_value)
```

```python
import functools
import math

import jax
import jax.numpy as jnp
from jax import lax
from jax.experimental import pallas as pl
from jax.experimental.pallas import tpu as pltpu
from jax.sharding import PartitionSpec as P

HEADS = 8
CHUNKS = 4
BIG = 1e30
MESH = pl.DeviceIdType.MESH
SLOT_OF_KIND = (2, 0, 4, 5, 3)
KIND_OF_SLOT = {2: 0, 0: 1, 4: 2, 5: 3, 3: 4}


def kernel(
    frames, blocks, block_len, head_dim,
    k_in, v_in, q_in, g_in, mask_ref, valid_ref,
    dq_ref, dk_ref, dv_ref,
    buf, bias, stat_in, stat_out, local_sem, send_sem, recv_sem, stat_send, stat_recv,
):
    inputs = (k_in, v_in, q_in, g_in)
    t = lax.axis_index("tm")
    s = lax.axis_index("seq")
    per_chunk = HEADS // CHUNKS
    width = per_chunk * head_dim
    scale = head_dim ** (-0.5)
    scale2 = scale * math.log2(math.e)
    has = {-1: s > 0, 1: s < blocks - 1}
    earlier, later = t > 0, t < frames - 1

    def rows(slot):
        return pl.ds(slot * block_len, block_len)

    def cols(c):
        return pl.ds(pl.multiple_of(c * width, width), width)

    def both(*conds):
        out = conds[0]
        for cond in conds[1:]:
            out = jnp.logical_and(out, cond)
        return out

    def copy(k, kind, c):
        slot = SLOT_OF_KIND[kind]
        src = inputs[k].at[0, :, cols(c)] if kind < 3 else buf.at[k, rows(4), cols(c)]
        if kind == 2:
            device = (t + 1, s) if k < 2 else (t - 1, s)
        else:
            device = (t, s - 1) if kind in (0, 3) else (t, s + 1)
        return pltpu.make_async_remote_copy(
            src_ref=src,
            dst_ref=buf.at[k, rows(slot), cols(c)],
            send_sem=send_sem.at[k, kind, c],
            recv_sem=recv_sem.at[k, slot, c],
            device_id=device,
            device_id_type=MESH,
        )

    def sends(k, kind):
        if kind == 2:
            return later if k < 2 else earlier
        side = has[-1] if kind in (0, 3) else has[1]
        if kind < 3:
            return side
        return both(side, earlier if k < 2 else later)

    def arrives(k, slot):
        conds = []
        if slot % 3 == 0:
            conds.append(has[-1])
        if slot % 3 == 2:
            conds.append(has[1])
        if slot >= 3:
            conds.append(earlier if k < 2 else later)
        return both(*conds)

    def stat_copy(f, d, c):
        slot = 3 * f + 1 - d
        return pltpu.make_async_remote_copy(
            src_ref=stat_out.at[slot, c],
            dst_ref=stat_in.at[slot, c],
            send_sem=stat_send.at[slot, c],
            recv_sem=stat_recv.at[slot, c],
            device_id=(t - f, s + d),
            device_id_type=MESH,
        )

    stat_targets = [(0, -1), (0, 1), (1, 0), (1, -1), (1, 1)]

    def stat_sends(f, d):
        conds = []
        if d:
            conds.append(has[d])
        if f:
            conds.append(earlier)
        return both(*conds)

    barrier = pltpu.get_barrier_semaphore()
    expected = jnp.int32(0)
    for dt in (-1, 0, 1):
        for ds in (-1, 0, 1):
            if dt == 0 and ds == 0:
                continue
            conds = []
            if dt:
                conds.append(earlier if dt < 0 else later)
            if ds:
                conds.append(has[ds])
            there = both(*conds)
            expected = expected + there.astype(jnp.int32)

            @pl.when(there)
            def _(dt=dt, ds=ds):
                pl.semaphore_signal(
                    barrier, inc=1, device_id=(t + dt, s + ds), device_id_type=MESH
                )

    own = [
        pltpu.make_async_copy(inputs[k].at[0], buf.at[k, rows(1), :], local_sem.at[k])
        for k in range(4)
    ]
    for c in own:
        c.start()
    pl.semaphore_wait(barrier, expected)

    for group in ((0, 1), (2, 3)):
        @pl.loop(0, CHUNKS)
        def _(c, group=group):
            for kind in (2, 0, 1):
                for k in group:
                    @pl.when(sends(k, kind))
                    def _(k=k, kind=kind):
                        copy(k, kind, c).start()

    for slot in (0, 2, 3, 4, 5):
        for k in range(4):
            @pl.when(jnp.logical_not(arrives(k, slot)))
            def _(k=k, slot=slot):
                buf[k, slot * block_len:(slot + 1) * block_len, :] = jnp.zeros(
                    (block_len, buf.shape[2]), buf.dtype
                )

        @pl.when(jnp.logical_not(arrives(2, slot)))
        def _(slot=slot):
            stat_in[slot] = jnp.full(stat_in.shape[1:], BIG, jnp.float32)

    key_pos = lax.broadcasted_iota(jnp.int32, (block_len, head_dim), 0)
    before = jnp.maximum(t - 1, 0)
    for cand in range(6):
        near = s + cand % 3 - 1
        conds = [jnp.logical_and(near >= 0, near < blocks)]
        frame_valid = valid_ref[t]
        if cand >= 3:
            conds.append(earlier)
            frame_valid = valid_ref[before]
        limit = frame_valid - near * block_len
        chosen = jnp.where(mask_ref[0, 0, cand] == 1, 1, 0) * both(*conds).astype(jnp.int32)
        limit = jnp.maximum(limit, 0) * chosen
        bias[cand * block_len:(cand + 1) * block_len, :] = jnp.where(key_pos < limit, 0.0, -BIG)

    own_limit = valid_ref[t] - s * block_len
    lane = lax.broadcasted_iota(jnp.int32, (1, block_len), 1)
    query_ok = lane < own_limit
    okay = jnp.where(query_ok, 1.0, 0.0)
    for c in own:
        c.wait()

    def relay(c, group):
        for k in group:
            @pl.when(earlier if k < 2 else later)
            def _(k=k):
                copy(k, 2, c).wait_recv()
                for kind in (3, 4):
                    @pl.when(sends(k, kind))
                    def _(kind=kind):
                        copy(k, kind, c).start()

    def await_sides(c, group):
        for slot in (0, 2, 3, 5):
            for k in group:
                @pl.when(arrives(k, slot))
                def _(k=k, slot=slot):
                    copy(k, KIND_OF_SLOT[slot], c).wait_recv()

    own_rows = slice(block_len, 2 * block_len)
    nt = (((1,), (1,)), ((), ()))
    tn = (((0,), (0,)), ((), ()))
    nn = (((1,), (0,)), ((), ()))

    def dot(a, b, dims):
        return lax.dot_general(a, b, dims, preferred_element_type=jnp.float32)

    def forward(c):
        await_sides(c, (0, 1))
        lses, dots = [], []
        for h in range(per_chunk):
            hc = pl.ds(pl.multiple_of(c * width + h * head_dim, head_dim), head_dim)
            key = buf[0, :, hc]
            value = buf[1, :, hc]
            query = buf[2, own_rows, hc]
            grad = buf[3, own_rows, hc]
            score = dot(key, query, nt) * scale2 + bias[...]
            peak = jnp.max(score, axis=0, keepdims=True)
            e = jnp.exp2(score - peak)
            total = jnp.sum(e, axis=0, keepdims=True)
            dprob = dot(value, grad, nt)
            norm = okay / total
            row_dot = jnp.sum(e * dprob, axis=0, keepdims=True) * norm
            dscore = (e * norm * (dprob - row_dot)).astype(jnp.bfloat16)
            dq = dot(dscore, key, tn) * scale
            dq_ref[0, :, hc] = dq.astype(dq_ref.dtype)
            lses.append(jnp.where(query_ok, peak + jnp.log2(total), BIG))
            dots.append(row_dot)
        for f, d in stat_targets + [(0, 0)]:
            slot = 3 * f + 1 - d
            cand = 3 * f + d + 1
            gate = jnp.where(mask_ref[0, 0, cand] == 1, 0.0, BIG)
            dest = stat_in if (f, d) == (0, 0) else stat_out
            for h in range(per_chunk):
                dest[slot, c, h:h + 1, :] = lses[h] + gate
                dest[slot, c, per_chunk + h:per_chunk + h + 1, :] = dots[h]
        for f, d in stat_targets:
            @pl.when(stat_sends(f, d))
            def _(f=f, d=d):
                stat_copy(f, d, c).start()

    @pl.loop(0, CHUNKS + 1)
    def _(c):
        @pl.when(c < CHUNKS)
        def _():
            relay(c, (0, 1))

        @pl.when(c > 0)
        def _():
            forward(c - 1)

        @pl.when(c < CHUNKS)
        def _():
            relay(c, (2, 3))

    key_ok = lax.broadcasted_iota(jnp.int32, (block_len, head_dim), 0) < own_limit

    @pl.loop(0, CHUNKS)
    def _(c):
        await_sides(c, (2, 3))
        for f, d in stat_targets:
            slot = 3 * f + 1 - d

            @pl.when(arrives(2, slot))
            def _(f=f, d=d):
                stat_copy(f, d, c).wait_recv()
        for h in range(per_chunk):
            hc = pl.ds(pl.multiple_of(c * width + h * head_dim, head_dim), head_dim)
            query = buf[2, :, hc]
            grad = buf[3, :, hc]
            key = buf[0, own_rows, hc]
            value = buf[1, own_rows, hc]
            lse = jnp.concatenate([stat_in[j, c, h:h + 1, :] for j in range(6)], axis=1)
            row_dot = jnp.concatenate(
                [stat_in[j, c, per_chunk + h:per_chunk + h + 1, :] for j in range(6)], axis=1
            )
            prob = jnp.exp2(dot(key, query, nt) * scale2 - lse)
            dprob = dot(value, grad, nt)
            dscore = (prob * (dprob - row_dot)).astype(jnp.bfloat16)
            dk = dot(dscore, query, nn) * scale
            dv = dot(prob.astype(jnp.bfloat16), grad, nn)
            dk_ref[0, :, hc] = jnp.where(key_ok, dk, 0.0).astype(dk_ref.dtype)
            dv_ref[0, :, hc] = jnp.where(key_ok, dv, 0.0).astype(dv_ref.dtype)

    @pl.loop(0, CHUNKS)
    def _(c):
        for k in range(4):
            for kind in range(5):
                @pl.when(sends(k, kind))
                def _(k=k, kind=kind):
                    copy(k, kind, c).wait_send()
        for f, d in stat_targets:
            @pl.when(stat_sends(f, d))
            def _(f=f, d=d):
                stat_copy(f, d, c).wait_send()


def solution(mesh):
    frames, blocks = mesh.shape["tm"], mesh.shape["seq"]

    def body(queries, keys, values, grad_out, block_mask, valid_len):
        _, block_len, feat = queries.shape
        out = jax.ShapeDtypeStruct(queries.shape, queries.dtype)
        vmem = pl.BlockSpec(memory_space=pltpu.VMEM)
        smem = pl.BlockSpec(memory_space=pltpu.SMEM)
        hbm = pl.BlockSpec(memory_space=pl.ANY)
        return pl.pallas_call(
            functools.partial(kernel, frames, blocks, block_len, feat // HEADS),
            out_shape=(out, out, out),
            in_specs=[hbm] * 4 + [smem] * 2,
            out_specs=(vmem,) * 3,
            scratch_shapes=[
                pltpu.VMEM((4, 6 * block_len, feat), jnp.bfloat16),
                pltpu.VMEM((6 * block_len, block_len), jnp.float32),
                pltpu.VMEM((6, CHUNKS, 8, block_len), jnp.float32),
                pltpu.VMEM((6, CHUNKS, 8, block_len), jnp.float32),
                pltpu.SemaphoreType.DMA((4,)),
                pltpu.SemaphoreType.DMA((4, 5, CHUNKS)),
                pltpu.SemaphoreType.DMA((4, 6, CHUNKS)),
                pltpu.SemaphoreType.DMA((6, CHUNKS)),
                pltpu.SemaphoreType.DMA((6, CHUNKS)),
            ],
            compiler_params=pltpu.CompilerParams(collective_id=0, has_side_effects=True),
        )(keys, values, queries, grad_out, block_mask, valid_len)

    spec = P("tm", "seq", None)
    return jax.shard_map(
        body, mesh=mesh, in_specs=(spec,) * 5 + (P(),), out_specs=(spec,) * 3, check_vma=False
    )
```

```python
import functools
import math

import jax
import jax.numpy as jnp
from jax import lax
from jax.experimental import pallas as pl
from jax.experimental.pallas import tpu as pltpu
from jax.sharding import PartitionSpec as P

HEADS = 8
CHUNKS = 2
BIG = 1e30
MESH = pl.DeviceIdType.MESH
SLOT_OF_KIND = (2, 0, 4, 5, 3)
KIND_OF_SLOT = {2: 0, 0: 1, 4: 2, 5: 3, 3: 4}


def kernel(
    frames, blocks, block_len, head_dim,
    k_in, v_in, q_in, g_in, mask_ref, valid_ref,
    dq_ref, dk_ref, dv_ref,
    buf, bias, corner, corner_send, corner_recv, stat_in, stat_out, local_sem, send_sem, recv_sem, stat_send, stat_recv,
):
    inputs = (k_in, v_in, q_in, g_in)
    t = lax.axis_index("tm")
    s = lax.axis_index("seq")
    per_chunk = HEADS // CHUNKS
    width = per_chunk * head_dim
    scale = head_dim ** (-0.5)
    scale2 = scale * math.log2(math.e)
    has = {-1: s > 0, 1: s < blocks - 1}
    earlier, later = t > 0, t < frames - 1

    def rows(slot):
        return pl.ds(slot * block_len, block_len)

    def cols(c):
        return pl.ds(pl.multiple_of(c * width, width), width)

    def both(*conds):
        out = conds[0]
        for cond in conds[1:]:
            out = jnp.logical_and(out, cond)
        return out

    def copy(k, kind, c):
        slot = SLOT_OF_KIND[kind]
        src = inputs[k].at[0, :, cols(c)] if kind < 3 else buf.at[k, rows(4), cols(c)]
        if kind == 2:
            device = (t + 1, s) if k < 2 else (t - 1, s)
        else:
            device = (t, s - 1) if kind in (0, 3) else (t, s + 1)
        return pltpu.make_async_remote_copy(
            src_ref=src,
            dst_ref=buf.at[k, rows(slot), cols(c)],
            send_sem=send_sem.at[k, kind, c],
            recv_sem=recv_sem.at[k, slot, c],
            device_id=device,
            device_id_type=MESH,
        )

    square = frames == 4
    last = CHUNKS - 1

    def source(k):
        return t == (1 if k < 2 else 2)

    def at_corner(k):
        return t == (3 if k < 2 else 0)

    def hop(k):
        return pltpu.make_async_remote_copy(
            src_ref=inputs[k].at[0, :, last * width:],
            dst_ref=corner.at[k % 2],
            send_sem=send_sem.at[k, 2, last],
            recv_sem=corner_recv.at[k % 2],
            device_id=(t + 2, s) if k < 2 else (t - 2, s),
            device_id_type=MESH,
        )

    def onward(k):
        return pltpu.make_async_remote_copy(
            src_ref=corner.at[k % 2],
            dst_ref=buf.at[k, rows(4), last * width:],
            send_sem=corner_send.at[k % 2],
            recv_sem=recv_sem.at[k, 4, last],
            device_id=(t - 1, s) if k < 2 else (t + 1, s),
            device_id_type=MESH,
        )

    def sends(k, kind):
        if kind == 2:
            return later if k < 2 else earlier
        side = has[-1] if kind in (0, 3) else has[1]
        if kind < 3:
            return side
        return both(side, earlier if k < 2 else later)

    def arrives(k, slot):
        conds = []
        if slot % 3 == 0:
            conds.append(has[-1])
        if slot % 3 == 2:
            conds.append(has[1])
        if slot >= 3:
            conds.append(earlier if k < 2 else later)
        return both(*conds)

    def stat_copy(f, d, c):
        slot = 3 * f + 1 - d
        return pltpu.make_async_remote_copy(
            src_ref=stat_out.at[slot, c],
            dst_ref=stat_in.at[slot, c],
            send_sem=stat_send.at[slot, c],
            recv_sem=stat_recv.at[slot, c],
            device_id=(t - f, s + d),
            device_id_type=MESH,
        )

    stat_targets = [(0, -1), (0, 1), (1, 0), (1, -1), (1, 1)]

    def stat_sends(f, d):
        conds = []
        if d:
            conds.append(has[d])
        if f:
            conds.append(earlier)
        return both(*conds)

    barrier = pltpu.get_barrier_semaphore()
    expected = jnp.int32(0)
    for dt in (-1, 0, 1):
        for ds in (-1, 0, 1):
            if dt == 0 and ds == 0:
                continue
            conds = []
            if dt:
                conds.append(earlier if dt < 0 else later)
            if ds:
                conds.append(has[ds])
            there = both(*conds)
            expected = expected + there.astype(jnp.int32)

            @pl.when(there)
            def _(dt=dt, ds=ds):
                pl.semaphore_signal(
                    barrier, inc=1, device_id=(t + dt, s + ds), device_id_type=MESH
                )

    if square:
        opposite = lax.rem(t + 2, frames)
        pl.semaphore_signal(barrier, inc=1, device_id=(opposite, s), device_id_type=MESH)
        expected = expected + 1

    own = [
        pltpu.make_async_copy(inputs[k].at[0], buf.at[k, rows(1), :], local_sem.at[k])
        for k in range(4)
    ]
    for c in own:
        c.start()
    pl.semaphore_wait(barrier, expected)

    for group, kinds in (((0, 1, 2, 3), (2,)), ((0, 1), (0, 1)), ((2, 3), (0, 1))):
        @pl.loop(0, CHUNKS)
        def _(c, group=group, kinds=kinds):
            for kind in kinds:
                for k in group:
                    there = sends(k, kind)
                    if kind == 2 and square:
                        round_corner = both(source(k), c == last)
                        there = both(there, jnp.logical_not(round_corner))

                        @pl.when(round_corner)
                        def _(k=k):
                            hop(k).start()

                    @pl.when(there)
                    def _(k=k, kind=kind):
                        copy(k, kind, c).start()

    for slot in (0, 2, 3, 4, 5):
        for k in range(4):
            @pl.when(jnp.logical_not(arrives(k, slot)))
            def _(k=k, slot=slot):
                buf[k, slot * block_len:(slot + 1) * block_len, :] = jnp.zeros(
                    (block_len, buf.shape[2]), buf.dtype
                )

        @pl.when(jnp.logical_not(arrives(2, slot)))
        def _(slot=slot):
            stat_in[slot] = jnp.full(stat_in.shape[1:], BIG, jnp.float32)

    key_pos = lax.broadcasted_iota(jnp.int32, (block_len, head_dim), 0)
    before = jnp.maximum(t - 1, 0)
    for cand in range(6):
        near = s + cand % 3 - 1
        conds = [jnp.logical_and(near >= 0, near < blocks)]
        frame_valid = valid_ref[t]
        if cand >= 3:
            conds.append(earlier)
            frame_valid = valid_ref[before]
        limit = frame_valid - near * block_len
        chosen = jnp.where(mask_ref[0, 0, cand] == 1, 1, 0) * both(*conds).astype(jnp.int32)
        limit = jnp.maximum(limit, 0) * chosen
        bias[cand * block_len:(cand + 1) * block_len, :] = jnp.where(key_pos < limit, 0.0, -BIG)

    own_limit = valid_ref[t] - s * block_len
    lane = lax.broadcasted_iota(jnp.int32, (1, block_len), 1)
    query_ok = lane < own_limit
    okay = jnp.where(query_ok, 1.0, 0.0)
    for c in own:
        c.wait()

    def relay(c, group):
        for k in group:
            @pl.when(earlier if k < 2 else later)
            def _(k=k):
                copy(k, 2, c).wait_recv()
                for kind in (3, 4):
                    @pl.when(sends(k, kind))
                    def _(kind=kind):
                        copy(k, kind, c).start()

    def await_sides(c, group):
        for slot in (0, 2, 3, 5):
            for k in group:
                @pl.when(arrives(k, slot))
                def _(k=k, slot=slot):
                    copy(k, KIND_OF_SLOT[slot], c).wait_recv()

    own_rows = slice(block_len, 2 * block_len)
    nt = (((1,), (1,)), ((), ()))
    tn = (((0,), (0,)), ((), ()))
    nn = (((1,), (0,)), ((), ()))

    def dot(a, b, dims):
        return lax.dot_general(a, b, dims, preferred_element_type=jnp.float32)

    def forward(c):
        await_sides(c, (0, 1))
        lses, dots = [], []
        for h in range(per_chunk):
            hc = pl.ds(pl.multiple_of(c * width + h * head_dim, head_dim), head_dim)
            key = buf[0, :, hc]
            value = buf[1, :, hc]
            query = buf[2, own_rows, hc]
            grad = buf[3, own_rows, hc]
            score = dot(key, query, nt) * scale2 + bias[...]
            peak = jnp.max(score, axis=0, keepdims=True)
            e = jnp.exp2(score - peak)
            total = jnp.sum(e, axis=0, keepdims=True)
            dprob = dot(value, grad, nt)
            norm = okay / total
            row_dot = jnp.sum(e * dprob, axis=0, keepdims=True) * norm
            dscore = (e * norm * (dprob - row_dot)).astype(jnp.bfloat16)
            dq = dot(dscore, key, tn) * scale
            dq_ref[0, :, hc] = dq.astype(dq_ref.dtype)
            lses.append(jnp.where(query_ok, peak + jnp.log2(total), BIG))
            dots.append(row_dot)
        for f, d in stat_targets + [(0, 0)]:
            slot = 3 * f + 1 - d
            cand = 3 * f + d + 1
            gate = jnp.where(mask_ref[0, 0, cand] == 1, 0.0, BIG)
            dest = stat_in if (f, d) == (0, 0) else stat_out
            for h in range(per_chunk):
                dest[slot, c, h:h + 1, :] = lses[h] + gate
                dest[slot, c, per_chunk + h:per_chunk + h + 1, :] = dots[h]
        for f, d in stat_targets:
            @pl.when(stat_sends(f, d))
            def _(f=f, d=d):
                stat_copy(f, d, c).start()

    @pl.loop(0, CHUNKS + 1)
    def _(c):
        @pl.when(c < CHUNKS)
        def _():
            relay(c, (0, 1))

        @pl.when(c > 0)
        def _():
            forward(c - 1)

        @pl.when(c < CHUNKS)
        def _():
            relay(c, (2, 3))

        if square:
            for group in ((0, 1), (2, 3)):
                @pl.when(both(at_corner(group[0]), c == 0))
                def _(group=group):
                    for k in group:
                        hop(k).wait_recv()
                        onward(k).start()

    key_ok = lax.broadcasted_iota(jnp.int32, (block_len, head_dim), 0) < own_limit

    @pl.loop(0, CHUNKS)
    def _(c):
        await_sides(c, (2, 3))
        for f, d in stat_targets:
            slot = 3 * f + 1 - d

            @pl.when(arrives(2, slot))
            def _(f=f, d=d):
                stat_copy(f, d, c).wait_recv()
        for h in range(per_chunk):
            hc = pl.ds(pl.multiple_of(c * width + h * head_dim, head_dim), head_dim)
            query = buf[2, :, hc]
            grad = buf[3, :, hc]
            key = buf[0, own_rows, hc]
            value = buf[1, own_rows, hc]
            lse = jnp.concatenate([stat_in[j, c, h:h + 1, :] for j in range(6)], axis=1)
            row_dot = jnp.concatenate(
                [stat_in[j, c, per_chunk + h:per_chunk + h + 1, :] for j in range(6)], axis=1
            )
            prob = jnp.exp2(dot(key, query, nt) * scale2 - lse)
            dprob = dot(value, grad, nt)
            dscore = (prob * (dprob - row_dot)).astype(jnp.bfloat16)
            dk = dot(dscore, query, nn) * scale
            dv = dot(prob.astype(jnp.bfloat16), grad, nn)
            dk_ref[0, :, hc] = jnp.where(key_ok, dk, 0.0).astype(dk_ref.dtype)
            dv_ref[0, :, hc] = jnp.where(key_ok, dv, 0.0).astype(dv_ref.dtype)

    @pl.loop(0, CHUNKS)
    def _(c):
        for k in range(4):
            for kind in range(5):
                @pl.when(sends(k, kind))
                def _(k=k, kind=kind):
                    copy(k, kind, c).wait_send()
        for f, d in stat_targets:
            @pl.when(stat_sends(f, d))
            def _(f=f, d=d):
                stat_copy(f, d, c).wait_send()
    if square:
        for group in ((0, 1), (2, 3)):
            @pl.when(at_corner(group[0]))
            def _(group=group):
                for k in group:
                    onward(k).wait_send()


def solution(mesh):
    frames, blocks = mesh.shape["tm"], mesh.shape["seq"]

    def body(queries, keys, values, grad_out, block_mask, valid_len):
        _, block_len, feat = queries.shape
        out = jax.ShapeDtypeStruct(queries.shape, queries.dtype)
        vmem = pl.BlockSpec(memory_space=pltpu.VMEM)
        smem = pl.BlockSpec(memory_space=pltpu.SMEM)
        hbm = pl.BlockSpec(memory_space=pl.ANY)
        return pl.pallas_call(
            functools.partial(kernel, frames, blocks, block_len, feat // HEADS),
            out_shape=(out, out, out),
            in_specs=[hbm] * 4 + [smem] * 2,
            out_specs=(vmem,) * 3,
            scratch_shapes=[
                pltpu.VMEM((4, 6 * block_len, feat), jnp.bfloat16),
                pltpu.VMEM((6 * block_len, block_len), jnp.float32),
                pltpu.VMEM((2, block_len, feat // CHUNKS), jnp.bfloat16),
                pltpu.SemaphoreType.DMA((2,)),
                pltpu.SemaphoreType.DMA((2,)),
                pltpu.VMEM((6, CHUNKS, 16, block_len), jnp.float32),
                pltpu.VMEM((6, CHUNKS, 16, block_len), jnp.float32),
                pltpu.SemaphoreType.DMA((4,)),
                pltpu.SemaphoreType.DMA((4, 5, CHUNKS)),
                pltpu.SemaphoreType.DMA((4, 6, CHUNKS)),
                pltpu.SemaphoreType.DMA((6, CHUNKS)),
                pltpu.SemaphoreType.DMA((6, CHUNKS)),
            ],
            compiler_params=pltpu.CompilerParams(collective_id=0, has_side_effects=True),
        )(keys, values, queries, grad_out, block_mask, valid_len)

    spec = P("tm", "seq", None)
    return jax.shard_map(
        body, mesh=mesh, in_specs=(spec,) * 5 + (P(),), out_specs=(spec,) * 3, check_vma=False
    )
```
